32 devices in a mesh: grp: 4 (over y, core), sp: 4 (over z), tp: 2 (over x).
Axes of the slice: x: 2, y: 2, z: 4, core: 2. Of those that a mesh axis runs over, the one named last changes fastest.
Arguments:
- queries: bfloat16 [4, 768, 2560], P('grp', 'sp', 'tp'), may hold values from -60 to 60
- key_tokens: bfloat16 [4, 768, 2560], P('grp', 'sp', 'tp'), may hold values from -60 to 60
- value_tokens: bfloat16 [4, 768, 2560], P('grp', 'sp', 'tp'), may hold values from -6 to 6
- norm_gains: float32 [2, 2560], P(None, 'grp'), may hold values from 0.25 to 1.75
- lengths: int32 [4], P('grp'), may hold values from 192 to 768
Outputs:
- attended: bfloat16 [4, 768, 2560], P('grp', 'sp', 'tp')
The draws below stay inside these ranges and needn't reach their ends.
All inputs are finite; a program needn't handle non-finite values.
Results may differ from the reference program's by a relative error of at most 0.011.
Values may be sent and summed in bfloat16 or wider, within the bound.
No kernel may reach another device: no remote copies, remote signals or barrier semaphores. Data moves between devices by JAX's collectives and lax.ppermute only.
A program may use at most 64 MiB of HBM per device.

```python
import math
import jax
import jax.numpy as jnp
from jax import lax

HEADS = 20
HEAD_DIM = 128
FEATURES = 2560
LENGTH = 768
SEQS = 4


def scaled_log(source, extent, lowest, highest):
    return jnp.exp(jax.random.uniform(source, extent, jnp.float32, math.log(lowest), math.log(highest)))


def paired_fields(key):
    full_shape = (SEQS, LENGTH, FEATURES)
    column_ramp = jnp.sqrt(1.0 + 2.0 * jnp.arange(FEATURES, dtype=jnp.float32) / (FEATURES - 1))
    query_base = jax.random.normal(jax.random.fold_in(key, 11), full_shape, jnp.float32)
    key_base = jax.random.normal(jax.random.fold_in(key, 12), full_shape, jnp.float32)
    row_scales = scaled_log(jax.random.fold_in(key, 14), (2, SEQS, LENGTH, 1), 0.3, 3.0)
    column_scales = column_ramp * scaled_log(jax.random.fold_in(key, 15), (2, 1, 1, FEATURES), 0.5, 2.0)
    query_rows = query_base * row_scales[0] * column_scales[0]
    key_rows = key_base * row_scales[1] * column_scales[1]
    return (jnp.clip(query_rows, -60.0, 60.0), jnp.clip(key_rows, -60.0, 60.0))


def draw_queries(key, part):
    return paired_fields(key)[0].astype(jnp.bfloat16)


def draw_key_tokens(key, part):
    return paired_fields(key)[1].astype(jnp.bfloat16)


def with_ends(values, key, least, top_value):
    place = [jax.random.randint(jax.random.fold_in(key, axis), (), 0, length) for axis, length in enumerate(values.shape)]
    main_axis = values.shape.index(max(values.shape))
    beside = place[:main_axis] + [(place[main_axis] + 1) % values.shape[main_axis]] + place[main_axis + 1:]
    return values.at[tuple(place)].set(least).at[tuple(beside)].set(top_value)


def block_levels(stream_key, shape, shards, least, high):
    loudness, own = 1.0, jax.random.fold_in(stream_key, 6)
    for position, blocks in shards:
        heights = jnp.exp(jax.random.uniform(jax.random.fold_in(own, position), (blocks,), jnp.float32, least / len(shards), high / len(shards)))
        loudness = loudness * jnp.repeat(heights, shape[position] // blocks).reshape([-1 if axis == position else 1 for axis in range(len(shape))])
    return loudness


def normal_values(rng, shape, scale, most, pieces=(), kind=jnp.bfloat16):
    array = jax.random.normal(rng, shape, jnp.float32) * scale
    if len(pieces) > 0:
        array = block_levels(rng, shape, pieces, -0.22, 0.18) * array
    return jnp.clip(array, min=-most, max=most).astype(kind)


def setup_inputs(seed: int = 0) -> dict:
    key_list = jax.random.split(jax.random.key(seed), 6)
    queries = draw_queries(jax.random.fold_in(key_list[5], 71), 0)
    key_tokens = draw_key_tokens(jax.random.fold_in(key_list[5], 71), 0)
    value_tokens = normal_values(key_list[2], (SEQS, LENGTH, FEATURES), 1.0, 6.0, ((0, 4), (1, 4), (2, 2)))
    norm_gains = jnp.clip(1.0 + 0.15 * jax.random.normal(key_list[3], (2, FEATURES), jnp.float32), 0.25, 1.75)
    lengths = with_ends(jax.random.randint(key_list[4], (SEQS,), LENGTH // 4, LENGTH + 1), jax.random.fold_in(key_list[4], 1), LENGTH // 4, LENGTH).astype(jnp.int32)
    return dict(queries=queries, key_tokens=key_tokens, value_tokens=value_tokens, norm_gains=norm_gains, lengths=lengths)


EPSILON = 1e-06
MASKED = -1e+30

def normalize(field, gains):
    widened = field.astype(jnp.float32)
    mean_square = lax.optimization_barrier(jnp.mean(widened * widened, axis=-1, keepdims=True))
    return (widened * lax.rsqrt(mean_square + EPSILON) * gains).astype(jnp.bfloat16)

def one_head(inputs):
    query_head, key_head, value_head, length = inputs
    scores = jnp.dot(query_head, key_head.T, preferred_element_type=jnp.float32) * (1.0 / math.sqrt(HEAD_DIM))
    visible = jnp.arange(LENGTH) < length
    scores = jnp.where(visible[None, :], scores, MASKED)
    largest = lax.optimization_barrier(jnp.max(scores, axis=-1, keepdims=True))
    weights = jnp.where(visible[None, :], jnp.exp(scores - largest), 0.0)
    denominator = lax.optimization_barrier(jnp.sum(weights, axis=-1, keepdims=True))
    numerator = jnp.dot(weights.astype(jnp.bfloat16), value_head, preferred_element_type=jnp.float32)
    return numerator / denominator

def by_heads(field):
    return field.reshape(LENGTH, HEADS, HEAD_DIM).transpose(1, 0, 2)

def one_sample(inputs):
    query_sample, key_sample, value_sample, length = inputs
    counts = jnp.broadcast_to(length, (HEADS,))
    result = lax.map(one_head, (by_heads(query_sample), by_heads(key_sample), by_heads(value_sample), counts))
    return result.transpose(1, 0, 2).reshape(LENGTH, FEATURES).astype(jnp.bfloat16)

def reference(queries, key_tokens, value_tokens, norm_gains, lengths):
    query_norm = normalize(queries, norm_gains[0])
    key_norm = normalize(key_tokens, norm_gains[1])
    return lax.map(one_sample, (query_norm, key_norm, value_tokens, lengths))
```

```python
import functools
import math

import jax
import jax.numpy as jnp
from jax import lax
from jax.experimental import pallas as pl
from jax.experimental.pallas import tpu as pltpu
from jax.sharding import PartitionSpec as P

HEAD_DIM = 128


EPSILON = 1e-06
MASKED = -1e30


def attend_block(running, query_heads, key_piece, value_piece, offset, length):
    largest, denominator, numerator = running
    row_count = key_piece.shape[0]
    heads_here = query_heads.shape[1]
    key_heads = key_piece.reshape(row_count, heads_here, HEAD_DIM)
    value_heads = value_piece.reshape(row_count, heads_here, HEAD_DIM)
    scores = jnp.einsum(
        "qhd,khd->hqk", query_heads, key_heads, preferred_element_type=jnp.float32
    ) * (1.0 / math.sqrt(HEAD_DIM))
    visible = offset + jnp.arange(row_count, dtype=jnp.int32) < length
    scores = jnp.where(visible[None, None, :], scores, MASKED)
    newest = jnp.maximum(largest, jnp.max(scores, axis=-1))
    weights = jnp.where(visible[None, None, :], jnp.exp(scores - newest[:, :, None]), 0.0)
    factor = jnp.exp(largest - newest)
    denominator = denominator * factor + jnp.sum(weights, axis=-1)
    update = jnp.einsum(
        "hqk,khd->qhd",
        weights.astype(jnp.bfloat16),
        value_heads,
        preferred_element_type=jnp.float32,
    )
    numerator = numerator * factor.T[:, :, None] + update
    return (newest, denominator, numerator)


def gathered_device(queries, key_tokens, value_tokens, norm_gains, lengths):
    query_rows = queries[0]
    key_rows = key_tokens[0]
    value_rows = value_tokens[0]
    length = lengths[0]
    query_wide = query_rows.astype(jnp.float32)
    key_wide = key_rows.astype(jnp.float32)
    query_square, key_square = lax.psum(
        (jnp.sum(query_wide * query_wide, axis=1), jnp.sum(key_wide * key_wide, axis=1)), "tp"
    )
    gathered_gains = lax.all_gather(norm_gains, "grp", axis=1, tiled=True)
    local_width = query_rows.shape[1]
    full_width = local_width * lax.axis_size("tp")
    local_gains = lax.dynamic_slice_in_dim(
        gathered_gains, lax.axis_index("tp") * local_width, local_width, 1
    )
    query_norm = (
        query_wide * lax.rsqrt(query_square / full_width + EPSILON)[:, None] * local_gains[0]
    ).astype(jnp.bfloat16)
    key_norm = (
        key_wide * lax.rsqrt(key_square / full_width + EPSILON)[:, None] * local_gains[1]
    ).astype(jnp.bfloat16)
    tokens_here = query_rows.shape[0]
    heads_here = local_width // HEAD_DIM
    query_heads = query_norm.reshape(tokens_here, heads_here, HEAD_DIM)
    initial = (
        jnp.full((heads_here, tokens_here), MASKED, jnp.float32),
        jnp.zeros((heads_here, tokens_here), jnp.float32),
        jnp.zeros((tokens_here, heads_here, HEAD_DIM), jnp.float32),
    )
    all_keys = lax.all_gather(key_norm, "sp", axis=0, tiled=True)
    all_values = lax.all_gather(value_rows, "sp", axis=0, tiled=True)
    total_rows = all_keys.shape[0]
    blocks_joined = 1
    while blocks_joined * tokens_here < 512 and blocks_joined < lax.axis_size("sp"):
        blocks_joined = blocks_joined * 2
    block_rows = blocks_joined * tokens_here

    def loop_body(block_index, running):
        first_row = block_index * block_rows
        key_block = lax.dynamic_slice_in_dim(all_keys, first_row, block_rows, 0)
        value_block = lax.dynamic_slice_in_dim(all_values, first_row, block_rows, 0)
        return attend_block(running, query_heads, key_block, value_block, first_row, length)

    final_state = lax.fori_loop(0, total_rows // block_rows, loop_body, initial)
    result = final_state[2] / final_state[1].T[:, :, None]
    return result.reshape(tokens_here, local_width).astype(jnp.bfloat16)[None]


def attend_kernel(
    q_own, q_near, k_own, v_own, k_far, v_far, near, far_near, row_scale, col_terms, gains,
    out_own, out_near, scale_cols,
):
    tokens = q_own.shape[1]
    rows = 2 * tokens

    @pl.when(pl.program_id(0) == 0)
    def _():
        spread = jnp.broadcast_to(row_scale[...], (HEAD_DIM, rows))
        scale_cols[...] = spread.T

    keys = jnp.concatenate([k_own[0], near[0], k_far[0], far_near[0]], axis=0)
    values = jnp.concatenate([v_own[0], near[1], v_far[0], far_near[1]], axis=0)
    values = jnp.concatenate([values, jnp.ones_like(values)], axis=1)
    key_scale = col_terms[0:1, :]
    key_bias = col_terms[1:2, :]
    for source, out, start in ((q_own, out_own, 0), (q_near, out_near, tokens)):
        query = source[0].astype(jnp.float32) * scale_cols[start : start + tokens, :]
        query = (query * gains[...]).astype(jnp.bfloat16)
        scores = lax.dot_general(
            query, keys, (((1,), (1,)), ((), ())), preferred_element_type=jnp.float32
        )
        scores = scores * key_scale + key_bias
        weights = jnp.exp2(scores - jnp.max(scores, axis=1, keepdims=True))
        result = jnp.dot(
            weights.astype(jnp.bfloat16), values, preferred_element_type=jnp.float32
        )
        out[...] = (result[:, :HEAD_DIM] / result[:, HEAD_DIM:]).astype(jnp.bfloat16)


def attend(first, count, q_own, q_near, k_own, v_own, k_far, v_far, near, far_near, row_scale,
           col_terms, gains):
    tokens = q_own.shape[1]
    keys = col_terms.shape[1]
    whole = pl.BlockSpec((1, tokens, HEAD_DIM), lambda i: (0, 0, first + i))
    part = pl.BlockSpec((2, tokens, HEAD_DIM), lambda i: (0, 0, i))
    out = pl.BlockSpec((tokens, HEAD_DIM), lambda i: (0, i))
    shape = jax.ShapeDtypeStruct((tokens, count * HEAD_DIM), jnp.bfloat16)
    return pl.pallas_call(
        attend_kernel,
        grid=(count,),
        in_specs=[whole] * 6 + [part] * 2 + [
            pl.BlockSpec(row_scale.shape, lambda i: (0, 0)),
            pl.BlockSpec(col_terms.shape, lambda i: (0, 0)),
            pl.BlockSpec((1, HEAD_DIM), lambda i: (0, first + i)),
        ],
        out_specs=[out, out],
        out_shape=[shape, shape],
        scratch_shapes=[pltpu.VMEM((2 * tokens, HEAD_DIM), jnp.float32)],
        cost_estimate=pl.CostEstimate(
            flops=8 * count * tokens * keys * HEAD_DIM,
            bytes_accessed=20 * count * tokens * HEAD_DIM * 2,
            transcendentals=2 * count * tokens * keys,
        ),
        name="attend",
    )(q_own, q_near, k_own, v_own, k_far, v_far, near, far_near, row_scale, col_terms, gains)


def head_chunks(heads):
    sizes = []
    while sum(sizes) < heads:
        sizes.append(min(max(1, (2 * heads) // 5), heads - sum(sizes)))
    return sizes


def hub_device(queries, key_tokens, value_tokens, norm_gains, lengths):
    inward = [(0, 1), (3, 2)]
    outward = [(1, 0), (2, 3)]
    across = [(1, 2), (2, 1)]
    place = lax.axis_index("sp")
    inner = (place == 1) | (place == 2)
    tokens, width = queries.shape[1:]
    heads = width // HEAD_DIM
    full_width = width * lax.axis_size("tp")

    v_far = lax.ppermute(value_tokens, "sp", across)
    k_far = lax.ppermute(key_tokens, "sp", across)
    chunks, first = [], 0
    for count in head_chunks(heads):
        cut = slice(first * HEAD_DIM, (first + count) * HEAD_DIM)
        packed = jnp.concatenate([key_tokens[:, :, cut], value_tokens[:, :, cut]], axis=0)
        near = lax.ppermute(packed, "sp", inward)
        far_near = lax.ppermute(near, "sp", across)
        chunks.append((first, count, near, far_near))
        first += count
    q_near = lax.ppermute(queries, "sp", inward)

    query_wide = queries[0].astype(jnp.float32)
    key_wide = key_tokens[0].astype(jnp.float32)
    squares = lax.psum(
        jnp.stack([jnp.sum(query_wide * query_wide, axis=1), jnp.sum(key_wide * key_wide, axis=1)]), "tp"
    )
    scales = lax.rsqrt(squares / full_width + EPSILON)
    near_scales = lax.ppermute(scales, "sp", inward)
    far_scales = lax.ppermute(jnp.stack([scales[1], near_scales[1]]), "sp", across)
    row_scale = jnp.concatenate([scales[0:1], near_scales[0:1]], axis=1)
    far_place = lax.axis_size("sp") - 1 - place
    blocks = jnp.stack([place, place ^ 1, far_place, far_place ^ 1])
    positions = (blocks[:, None] * tokens + jnp.arange(tokens, dtype=jnp.int32)[None, :]).reshape(1, -1)
    key_bias = jnp.where(positions < lengths[0], 0.0, MASKED)
    key_scale = jnp.concatenate([scales[1:2], near_scales[1:2], far_scales[0:1], far_scales[1:2]], axis=1)
    col_terms = jnp.concatenate([key_scale, key_bias], axis=0)

    gathered = lax.all_gather(norm_gains, "grp", axis=1, tiled=True)
    gains = lax.dynamic_slice_in_dim(gathered, lax.axis_index("tp") * width, width, 1)
    gains = gains[0:1] * gains[1:2] * (math.log2(math.e) / math.sqrt(HEAD_DIM))

    pieces = []
    for first, count, near, far_near in chunks:
        out_own, out_near = attend(
            first, count, queries, q_near, key_tokens, value_tokens, k_far, v_far, near, far_near,
            row_scale, col_terms, gains,
        )
        returned = lax.ppermute(out_near, "sp", outward)
        pieces.append(jnp.where(inner, out_own, returned))
    return jnp.concatenate(pieces, axis=1)[None]


def solution(mesh):
    placed = (
        P("grp", "sp", "tp"),
        P("grp", "sp", "tp"),
        P("grp", "sp", "tp"),
        P(None, "grp"),
        P("grp"),
    )
    per_device = hub_device if mesh.shape["sp"] == 4 else gathered_device
    return jax.shard_map(
        per_device, mesh=mesh, in_specs=placed, out_specs=P("grp", "sp", "tp"), check_vma=False
    )
```
